32 devices in a mesh: dp: 8 (over y, x, core), tensor: 4 (over z).
Axes of the slice: x: 2, y: 2, z: 4, core: 2. Of those that a mesh axis runs over, the one named last changes fastest.
Arguments:
- block_input: bfloat16 [4096, 1024], P('dp'), may hold values from -6 to 6
- cotangent: bfloat16 [4096, 1024], P('dp'), may hold values from -6 to 6
- seq_lengths: int32 [8, 4], P('dp'), may hold values from 0 to 512, as said below
- norm_gains: float32 [2, 2, 1024], replicated, may hold values from 0.1 to 1.9
- norm_biases: float32 [2, 2, 1024], replicated, may hold values from -3 to 3
- w_qkv: bfloat16 [2, 1024, 3, 1024], P(None, None, None, 'tensor'), may hold values from -0.1875 to 0.1875
- qv_bias: float32 [2, 2, 1024], P(None, None, 'tensor'), may hold values from -3 to 3
- w_out: bfloat16 [2, 1024, 1024], P(None, 'tensor'), may hold values from -0.375 to 0.375
- out_biases: float32 [2, 2, 1024], replicated, may hold values from -3 to 3
- w_up: bfloat16 [2, 1024, 4096], P(None, None, 'tensor'), may hold values from -0.1875 to 0.1875
- up_bias: float32 [2, 4096], P(None, 'tensor'), may hold values from -3 to 3
- w_down: bfloat16 [2, 4096, 1024], P(None, 'tensor'), may hold values from -0.09375 to 0.09375
Outputs:
- block_output: bfloat16 [4096, 1024], P('dp')
- input_grad: float32 [4096, 1024], P('dp')
- grad_norm_gains: float32 [2, 2, 1024], replicated
- grad_norm_biases: float32 [2, 2, 1024], replicated
- grad_w_qkv: float32 [2, 1024, 3, 1024], P(None, 'dp', None, 'tensor')
- grad_qv_bias: float32 [2, 2, 1024], P(None, None, 'tensor')
- grad_w_out: float32 [2, 1024, 1024], P(None, 'tensor', 'dp')
- grad_out_biases: float32 [2, 2, 1024], replicated
- grad_w_up: float32 [2, 1024, 4096], P(None, 'dp', 'tensor')
- grad_up_bias: float32 [2, 4096], P(None, 'tensor')
- grad_w_down: float32 [2, 4096, 1024], P(None, 'tensor', 'dp')
The draws below stay inside these ranges and needn't reach their ends.
Inputs may be any that keep to these rules, and one draw needn't show every extreme that they name: `seq_lengths`: each row's lengths sum to at most 512; zero lengths occur; in every draw one row holds a single sequence of exactly 512 tokens.
All inputs are finite; a program needn't handle non-finite values.
Results may differ from the reference program's by a relative error of at most 0.025.
Values may be sent and summed in bfloat16 or wider, within the bound.
A program may use at most 128 MiB of HBM per device.

```python
import jax
import jax.numpy as jnp
from jax import lax

D = 1024
HEADS = 16
HEAD_DIM = 64
FF = 4096
LAYERS = 2
SEQS = 4
TOK_DEV = 512
TOKENS = 4096
N_DP = 8
N_TENSOR = 4


def draw_seq_lengths(key, part):
    key_full, key_live, key_cuts = jax.random.split(key, 3)
    full_device = jax.random.randint(key_full, (), 0, N_DP)
    live_count = jax.random.randint(key_live, (N_DP,), TOK_DEV // 8, TOK_DEV + 1)
    is_full = jnp.arange(N_DP) == full_device
    live_count = jnp.where(is_full, TOK_DEV, live_count)
    cut_points = jax.random.randint(key_cuts, (N_DP, SEQS - 1), 0, TOK_DEV + 1) % (live_count[:, None] + 1)
    cut_points = jnp.where(is_full[:, None], TOK_DEV, jnp.sort(cut_points, axis=1))
    bounds = jnp.concatenate([jnp.zeros((N_DP, 1), jnp.int32), cut_points.astype(jnp.int32), live_count[:, None].astype(jnp.int32)], axis=1)
    return (bounds[:, 1:] - bounds[:, :-1]).astype(jnp.int32)


def shard_levels(rng, extent, cuts, smallest, top_value):
    def one(dim, shards_of):
        heights = jax.random.uniform(jax.random.fold_in(jax.random.fold_in(rng, 6), dim), (shards_of,), jnp.float32, smallest / len(cuts), top_value / len(cuts))
        return jnp.repeat(jnp.exp(heights), extent[dim] // shards_of).reshape((-1,) + (1,) * (len(extent) - dim - 1))

    level = one(*cuts[0])
    for cut in cuts[1:]:
        level = level * one(*cut)
    return level


def bell_draw(rng, dims, width, limit, cuts=(), kind=jnp.bfloat16):
    array = jax.random.normal(rng, dims, jnp.float32) * width
    if len(cuts) > 0:
        array = shard_levels(rng, dims, cuts, -0.22, 0.18) * array
    return jnp.clip(array, min=-limit, max=limit).astype(kind)


def setup_inputs(seed: int = 0) -> dict:
    arg_keys = jax.random.split(jax.random.key(seed), 13)
    return {
        "block_input": bell_draw(arg_keys[0], (TOKENS, D), 1.0, 6.0, ((0, 8),)),
        "cotangent": bell_draw(arg_keys[1], (TOKENS, D), 1.0, 6.0, ((0, 8),)),
        "seq_lengths": draw_seq_lengths(jax.random.fold_in(arg_keys[12], 71), 0),
        "norm_gains": jnp.clip(1.0 + 0.18 * jax.random.normal(arg_keys[3], (LAYERS, 2, D), jnp.float32), 0.1, 1.9),
        "norm_biases": bell_draw(arg_keys[4], (LAYERS, 2, D), 0.3, 3.0, (), jnp.float32),
        "w_qkv": bell_draw(arg_keys[5], (LAYERS, D, 3, D), D ** -0.5, 0.1875, ((3, 4),)),
        "qv_bias": bell_draw(arg_keys[6], (LAYERS, 2, D), 0.5, 3.0, ((2, 4),), jnp.float32),
        "w_out": bell_draw(arg_keys[7], (LAYERS, D, D), (D // 4) ** -0.5, 0.375, ((1, 4),)),
        "out_biases": bell_draw(arg_keys[8], (LAYERS, 2, D), 0.3, 3.0, (), jnp.float32),
        "w_up": bell_draw(arg_keys[9], (LAYERS, D, FF), D ** -0.5, 0.1875, ((2, 4),)),
        "up_bias": bell_draw(arg_keys[10], (LAYERS, FF), 0.5, 3.0, ((1, 4),), jnp.float32),
        "w_down": bell_draw(arg_keys[11], (LAYERS, FF, D), FF ** -0.5, 0.09375, ((1, 4),)),
    }


@jax.custom_vjp
def low(v):
    return lax.optimization_barrier(v.astype(jnp.bfloat16)).astype(jnp.float32)

@jax.custom_vjp
def low_back(v):
    return v

def low_keep(v):
    return (low(v), None)

def low_pass(kept, grad):
    return (grad,)

def back_keep(v):
    return (v, None)

def back_low(kept, grad):
    return (low(grad),)
low.defvjp(low_keep, low_pass)
low_back.defvjp(back_keep, back_low)
NORM_EPS = 1e-05
PRECISE = lax.Precision.HIGHEST

def layer_norm(residual, gain_vec, shift_vec):
    mean_row = lax.optimization_barrier(jnp.mean(residual, axis=-1, keepdims=True))
    centered = residual - mean_row
    variance = lax.optimization_barrier(jnp.mean(centered * centered, axis=-1, keepdims=True))
    return centered * lax.rsqrt(variance + NORM_EPS) * gain_vec + shift_vec

def gelu_tanh(pre_act):
    return 0.5 * pre_act * (1.0 + jnp.tanh(0.7978845608028654 * (pre_act + 0.044715 * pre_act * pre_act * pre_act)))

def segment_mask(lengths, row_count):
    seq_ends = jnp.cumsum(lengths).astype(jnp.int32)
    position = jnp.arange(row_count, dtype=jnp.int32)
    segment = lax.optimization_barrier(jnp.sum((position[:, None] >= seq_ends[None, :]).astype(jnp.int32), axis=1))
    same_seq = (segment[:, None] == segment[None, :]) & (position[None, :] <= position[:, None])
    row_gap = (position[:, None] - position[None, :]).astype(jnp.float32)
    live_rows = (position < seq_ends[-1]).astype(jnp.float32)
    return (same_seq, row_gap, live_rows)

def softmax_rows(scores):
    row_max = lax.optimization_barrier(jnp.max(scores, axis=-1, keepdims=True))
    log_total = row_max + jnp.log(lax.optimization_barrier(jnp.sum(jnp.exp(scores - row_max), axis=-1, keepdims=True)))
    return jnp.exp(scores - log_total)

def forward(residual, params, same_seq, row_gap):
    norm_gains, norm_biases, w_qkv, qv_bias, w_out, out_biases, w_up, up_bias, w_down = params
    shards = N_TENSOR
    local_width = D // shards
    heads_here = HEADS // shards
    hidden_here = FF // shards
    row_count = residual.shape[0]
    score_scale = HEAD_DIM ** (-0.5)
    slopes = jnp.exp2(-8.0 * (jnp.arange(HEADS, dtype=jnp.int32).astype(jnp.float32) + 1.0) / HEADS).reshape(shards, heads_here)
    for layer_idx in range(LAYERS):
        normed = low(layer_norm(residual, norm_gains[layer_idx, 0], norm_biases[layer_idx, 0]))
        copies = low_back(jnp.broadcast_to(normed, (shards, row_count, D)))
        weight = w_qkv[layer_idx].reshape(D, 3, shards, local_width)
        projected = jnp.einsum('ktd,dckn->kctn', copies, weight, precision=PRECISE)
        bias_pair = qv_bias[layer_idx].reshape(2, shards, local_width)
        queries = low(low_back(projected[:, 0] + bias_pair[0][:, None, :]))
        key_rows = low(low_back(projected[:, 1]))
        value_rows = low(low_back(projected[:, 2] + bias_pair[1][:, None, :]))
        query_heads = queries.reshape(shards, row_count, heads_here, HEAD_DIM)
        key_heads = key_rows.reshape(shards, row_count, heads_here, HEAD_DIM)
        value_heads = value_rows.reshape(shards, row_count, heads_here, HEAD_DIM)
        raw_scores = jnp.einsum('kthe,kshe->khts', query_heads, key_heads, precision=PRECISE) * score_scale
        raw_scores = raw_scores - slopes[:, :, None, None] * row_gap
        scores = jnp.where(same_seq, low_back(raw_scores), -1000000000.0)
        softmax_p = low(softmax_rows(scores))
        context = jnp.einsum('khts,kshe->kthe', softmax_p, value_heads, precision=PRECISE).reshape(shards, row_count, local_width)
        context = low(low_back(context))
        partial_value = jnp.einsum('ktn,knd->ktd', context, w_out[layer_idx].reshape(shards, local_width, D), precision=PRECISE)
        branch = low_back(lax.optimization_barrier(jnp.sum(low(partial_value), axis=0)))
        residual = residual + branch + out_biases[layer_idx, 0]
        normed = low(layer_norm(residual, norm_gains[layer_idx, 1], norm_biases[layer_idx, 1]))
        copies = low_back(jnp.broadcast_to(normed, (shards, row_count, D)))
        up_proj = jnp.einsum('ktd,dkf->ktf', copies, w_up[layer_idx].reshape(D, shards, hidden_here), precision=PRECISE)
        up_proj = low_back(up_proj + up_bias[layer_idx].reshape(shards, 1, hidden_here))
        activated = low(gelu_tanh(up_proj))
        partial_value = jnp.einsum('ktf,kfd->ktd', activated, w_down[layer_idx].reshape(shards, hidden_here, D), precision=PRECISE)
        branch = low_back(lax.optimization_barrier(jnp.sum(low(partial_value), axis=0)))
        residual = residual + branch + out_biases[layer_idx, 1]
    return residual

def reference(block_input, cotangent, seq_lengths, norm_gains, norm_biases, w_qkv, qv_bias, w_out, out_biases, w_up, up_bias, w_down):
    params = (norm_gains.astype(jnp.float32), norm_biases.astype(jnp.float32), w_qkv.astype(jnp.float32), qv_bias.astype(jnp.float32), w_out.astype(jnp.float32), out_biases.astype(jnp.float32), w_up.astype(jnp.float32), up_bias.astype(jnp.float32), w_down.astype(jnp.float32))
    inputs = block_input.reshape(N_DP, TOK_DEV, D)
    arriving = cotangent.reshape(N_DP, TOK_DEV, D)

    def per_device(sums_now, device_item):
        rows_in, grad_in, lengths = device_item
        same_seq, row_gap, live_rows = segment_mask(lengths, TOK_DEV)

        def run_layers(rows_f, params_f):
            return forward(rows_f, params_f, same_seq, row_gap)
        result, pull_back = jax.vjp(run_layers, rows_in.astype(jnp.float32), params)
        rows_grad, params_grad = pull_back(grad_in.astype(jnp.float32) * live_rows[:, None])
        sums_now = jax.tree.map(lambda left, right: left + right, sums_now, params_grad)
        return (sums_now, (result.astype(jnp.bfloat16), rows_grad))
    zero_grads = jax.tree.map(jnp.zeros_like, params)
    totals, (results, row_grads) = lax.scan(per_device, zero_grads, (inputs, arriving, seq_lengths))
    gain_grad, shift_grad, qkv_grad, qvb_grad, out_grad, outb_grad, up_grad, upb_grad, down_grad = totals
    return (results.reshape(TOKENS, D), row_grads.reshape(TOKENS, D), gain_grad, shift_grad, qkv_grad, qvb_grad, out_grad, outb_grad, up_grad, upb_grad, down_grad)
```

```python
import functools

import jax
import jax.numpy as jnp
from jax import lax
from jax.experimental import pallas as pl
from jax.experimental.pallas import tpu as pltpu
from jax.sharding import PartitionSpec as P

HEADS = 16
HEAD_DIM = 64


NORM_EPS = 1e-05


def layer_norm(residual, gain_vec, shift_vec):
    mean_row = jnp.mean(residual, axis=-1, keepdims=True)
    centered = residual - mean_row
    variance = jnp.mean(centered * centered, axis=-1, keepdims=True)
    return centered * lax.rsqrt(variance + NORM_EPS) * gain_vec + shift_vec


def gelu_tanh(pre_act):
    return (
        0.5
        * pre_act
        * (1.0 + jnp.tanh(0.7978845608028654 * (pre_act + 0.044715 * pre_act * pre_act * pre_act)))
    )


def norm_back(residual, gain_vec, shift_vec, grad_normed):
    result, pull_back = jax.vjp(layer_norm, residual, gain_vec, shift_vec)
    return pull_back(grad_normed)


def segment_mask(lengths, row_count):
    seq_ends = jnp.cumsum(lengths)
    position = jnp.arange(row_count, dtype=jnp.int32)
    segment = jnp.sum((position[:, None] >= seq_ends[None, :]).astype(jnp.int32), axis=1)
    same_seq = (segment[:, None] == segment[None, :]) & (position[None, :] <= position[:, None])
    row_gap = (position[:, None] - position[None, :]).astype(jnp.float32)
    live_rows = (position < seq_ends[-1]).astype(jnp.float32)
    return (same_seq, row_gap, live_rows)


MESH = pl.DeviceIdType.MESH
LAG = 3


def line_sum_kernel(n, p_ref, out_ref, rin, up, rx, up_send, in_recv, x_recv, out_send, out_recv):
    chunks = p_ref.shape[0]
    half = n // 2
    me = lax.axis_index("tensor")
    side = me // half
    step = 1 - 2 * side
    inward = me + step
    outward = me - step
    depth = side * (n - 1) + me * step

    barrier = pltpu.get_barrier_semaphore()
    pl.semaphore_signal(barrier, inc=1, device_id={"tensor": inward}, device_id_type=MESH)

    @pl.when(depth > 0)
    def _():
        pl.semaphore_signal(barrier, inc=1, device_id={"tensor": outward}, device_id_type=MESH)
        pl.semaphore_wait(barrier, 2)

    @pl.when(depth == 0)
    def _():
        pl.semaphore_wait(barrier, 1)

    def copy(source, target, send, recv, c, device):
        return pltpu.make_async_remote_copy(
            src_ref=source.at[c],
            dst_ref=target.at[c],
            send_sem=send.at[c],
            recv_sem=recv.at[c],
            device_id={"tensor": device},
            device_id_type=MESH,
        )

    def loop(body, start=0, stop=chunks):
        lax.fori_loop(start, stop, lambda c, carry: (body(c), carry)[1], 0)

    f32 = jnp.float32

    for role in range(half):
        depth_zero = role == 0
        middle = role == half - 1
        target, target_sem = (rx, x_recv) if middle else (rin, in_recv)
        source = p_ref if depth_zero else up

        def rise(c, depth_zero=depth_zero, source=source, target=target, target_sem=target_sem):
            if not depth_zero:
                copy(rin, rin, up_send, in_recv, c, outward).wait_recv()
                up[c] = (p_ref[c].astype(f32) + rin[c].astype(f32)).astype(up.dtype)
            copy(source, target, up_send, target_sem, c, inward).start()

        def fall(c, depth_zero=depth_zero, middle=middle, source=source):
            if middle:
                copy(rx, rx, up_send, x_recv, c, inward).wait_recv()
                out_ref[c] = (source[c].astype(f32) + rx[c].astype(f32)).astype(out_ref.dtype)
            else:
                copy(out_ref, out_ref, out_send, out_recv, c, inward).wait_recv()
            if not depth_zero:
                copy(out_ref, out_ref, out_send, out_recv, c, outward).start()

        def drain(c, depth_zero=depth_zero, source=source, target=target, target_sem=target_sem):
            copy(source, target, up_send, target_sem, c, inward).wait_send()
            if not depth_zero:
                copy(out_ref, out_ref, out_send, out_recv, c, outward).wait_send()

        @pl.when(depth == role)
        def _(middle=middle, rise=rise, fall=fall, drain=drain):
            if middle:
                loop(rise, 0, LAG)

                def both(c):
                    rise(c)
                    fall(c - LAG)

                loop(both, LAG, chunks)
                loop(fall, chunks - LAG, chunks)
            else:
                loop(rise)
                loop(fall)
            loop(drain)


def line_sum(partial, n):
    rows, width = partial.shape
    chunks = 16
    shape = (chunks, rows // chunks, width)
    scratch = pltpu.VMEM(shape, partial.dtype)
    sems = pltpu.SemaphoreType.DMA((chunks,))
    out = pl.pallas_call(
        functools.partial(line_sum_kernel, n),
        out_shape=jax.ShapeDtypeStruct(shape, partial.dtype),
        in_specs=[pl.BlockSpec(memory_space=pltpu.VMEM)],
        out_specs=pl.BlockSpec(memory_space=pltpu.VMEM),
        scratch_shapes=[scratch, scratch, scratch, sems, sems, sems, sems, sems],
        compiler_params=pltpu.CompilerParams(
            collective_id=0, has_side_effects=True, vmem_limit_bytes=12 << 20
        ),
        cost_estimate=pl.CostEstimate(
            flops=30 * 10**9, bytes_accessed=2 * rows * width * 2, transcendentals=0
        ),
        name="line_sum",
    )(partial.reshape(shape))
    return out.reshape(rows, width)


def small_sum_kernel(n, v_ref, out_ref, slots, send, recv):
    me = lax.axis_index("dp")
    barrier = pltpu.get_barrier_semaphore()
    for k in range(1, n):
        pl.semaphore_signal(
            barrier, inc=1, device_id={"dp": lax.rem(me + k, n)}, device_id_type=MESH
        )
    pl.semaphore_wait(barrier, n - 1)
    copies = []
    for k in range(1, n):
        copies.append(
            pltpu.make_async_remote_copy(
                src_ref=v_ref,
                dst_ref=slots.at[me],
                send_sem=send.at[k],
                recv_sem=recv.at[k],
                device_id={"dp": lax.rem(me + k, n)},
                device_id_type=MESH,
            )
        )
        copies[-1].start()
    slots[me] = v_ref[...]
    for k in range(1, n):
        pltpu.make_async_remote_copy(
            src_ref=v_ref,
            dst_ref=slots.at[lax.rem(me + n - k, n)],
            send_sem=send.at[k],
            recv_sem=recv.at[k],
            device_id={"dp": lax.rem(me + k, n)},
            device_id_type=MESH,
        ).wait_recv()
    total = slots[0].astype(jnp.float32)
    for k in range(1, n):
        total = total + slots[k].astype(jnp.float32)
    out_ref[...] = total
    for one in copies:
        one.wait_send()


def small_sum(values, n):
    return pl.pallas_call(
        functools.partial(small_sum_kernel, n),
        out_shape=jax.ShapeDtypeStruct(values.shape, jnp.float32),
        in_specs=[pl.BlockSpec(memory_space=pltpu.VMEM)],
        out_specs=pl.BlockSpec(memory_space=pltpu.VMEM),
        scratch_shapes=[
            pltpu.VMEM((n,) + values.shape, values.dtype),
            pltpu.SemaphoreType.DMA((n,)),
            pltpu.SemaphoreType.DMA((n,)),
        ],
        compiler_params=pltpu.CompilerParams(
            collective_id=1, has_side_effects=True, vmem_limit_bytes=8 << 20
        ),
        name="small_sum",
    )(values)


def on_device(
    n_dp,
    n_tensor,
    block_input,
    cotangent,
    seq_lengths,
    norm_gains,
    norm_biases,
    w_qkv,
    qv_bias,
    w_out,
    out_biases,
    w_up,
    up_bias,
    w_down,
):
    row_count = block_input.shape[0]
    my_rank = lax.axis_index("tensor")
    local_width = w_qkv.shape[3]
    heads_here = local_width // HEAD_DIM
    depth = w_qkv.shape[0]
    score_scale = HEAD_DIM ** (-0.5)
    f32 = jnp.float32
    same_seq, row_gap, live_rows = segment_mask(seq_lengths[0], row_count)
    head_index = my_rank * heads_here + jnp.arange(heads_here, dtype=jnp.int32) + 1
    slopes = jnp.exp2(-8.0 * head_index.astype(f32) / HEADS)

    def branch_total(partial_value):
        return line_sum(partial_value.astype(jnp.bfloat16), n_tensor).astype(jnp.float32)

    def input_total(partial_value):
        return line_sum(partial_value.astype(jnp.bfloat16), n_tensor).astype(jnp.float32)

    def dp_share(*grads):
        joined = jnp.concatenate([grad.astype(jnp.bfloat16) for grad in grads], axis=1)
        return lax.psum_scatter(joined, "dp", scatter_dimension=0, tiled=True)

    def score_block(queries, key_rows):
        raw_scores = (
            jnp.einsum("the,she->hts", queries, key_rows, preferred_element_type=f32) * score_scale
        )
        raw_scores = raw_scores - slopes[:, None, None] * row_gap
        return jnp.where(same_seq, raw_scores, -1000000000.0)

    head_shape = (row_count, heads_here, HEAD_DIM)
    w_rows = w_qkv.transpose(0, 2, 1, 3)
    residual = block_input.astype(f32)
    stored = []
    for layer_idx in range(depth):
        entering = residual
        normed = layer_norm(residual, norm_gains[layer_idx, 0], norm_biases[layer_idx, 0]).astype(
            jnp.bfloat16
        )
        projected = jnp.einsum("td,cdn->ctn", normed, w_rows[layer_idx], preferred_element_type=f32)
        queries = (projected[0] + qv_bias[layer_idx, 0]).astype(jnp.bfloat16).reshape(head_shape)
        key_rows = projected[1].astype(jnp.bfloat16).reshape(head_shape)
        value_rows = (
            (projected[2] + qv_bias[layer_idx, 1]).astype(jnp.bfloat16).reshape(head_shape)
        )
        scores = score_block(queries, key_rows)
        row_max = jnp.max(scores, axis=-1, keepdims=True)
        log_total = row_max + jnp.log(jnp.sum(jnp.exp(scores - row_max), axis=-1, keepdims=True))
        softmax_p = jnp.exp(scores - log_total).astype(jnp.bfloat16)
        context = jnp.einsum("hts,she->the", softmax_p, value_rows, preferred_element_type=f32)
        context = context.astype(jnp.bfloat16).reshape(row_count, local_width)
        partial_value = jnp.dot(context, w_out[layer_idx], preferred_element_type=f32)
        residual = residual + branch_total(partial_value) + out_biases[layer_idx, 0]
        middle = residual
        normed_mlp = layer_norm(
            residual, norm_gains[layer_idx, 1], norm_biases[layer_idx, 1]
        ).astype(jnp.bfloat16)
        up_proj = (
            jnp.dot(normed_mlp, w_up[layer_idx], preferred_element_type=f32) + up_bias[layer_idx]
        )
        activated = gelu_tanh(up_proj).astype(jnp.bfloat16)
        partial_value = jnp.dot(activated, w_down[layer_idx], preferred_element_type=f32)
        if layer_idx == depth - 1:
            total = lax.psum(partial_value.astype(jnp.bfloat16), "tensor").astype(f32)
        else:
            total = branch_total(partial_value)
        residual = residual + total + out_biases[layer_idx, 1]
        stored.append(
            (
                entering,
                normed,
                queries,
                key_rows,
                value_rows,
                log_total,
                context,
                middle,
                normed_mlp,
                up_proj,
                activated,
            )
        )
    block_rows = residual.astype(jnp.bfloat16)
    grad_rows = cotangent.astype(f32) * live_rows[:, None]
    small_parts = []
    heavy_parts = []
    for layer_idx in reversed(range(depth)):
        (
            entering,
            normed,
            queries,
            key_rows,
            value_rows,
            log_total,
            context,
            middle,
            normed_mlp,
            up_proj,
            activated,
        ) = stored[layer_idx]
        down_bias_grad = jnp.sum(grad_rows, axis=0)
        grad_low = grad_rows.astype(jnp.bfloat16)
        down_w_grad = jnp.einsum("td,tf->df", grad_low, activated, preferred_element_type=f32)
        act_grad = jnp.einsum("td,fd->tf", grad_low, w_down[layer_idx], preferred_element_type=f32)
        up_grad = jax.vjp(gelu_tanh, up_proj)[1](act_grad)[0].astype(jnp.bfloat16)
        up_bias_grad = jnp.sum(up_grad.astype(f32), axis=0)
        up_w_grad = jnp.einsum("td,tf->df", normed_mlp, up_grad, preferred_element_type=f32)
        mlp_sum = dp_share(up_w_grad, down_w_grad)
        normed_grad = input_total(
            jnp.einsum("tf,df->td", up_grad, w_up[layer_idx], preferred_element_type=f32)
        )
        middle_grad, gain_mlp, shift_mlp = norm_back(
            middle, norm_gains[layer_idx, 1], norm_biases[layer_idx, 1], normed_grad
        )
        grad_rows = grad_rows + middle_grad
        out_bias_grad = jnp.sum(grad_rows, axis=0)
        grad_low = grad_rows.astype(jnp.bfloat16)
        out_w_grad = jnp.einsum("td,tn->dn", grad_low, context, preferred_element_type=f32)
        context_grad = jnp.einsum(
            "td,nd->tn", grad_low, w_out[layer_idx], preferred_element_type=f32
        )
        context_grad = context_grad.astype(jnp.bfloat16).reshape(head_shape)
        scores = score_block(queries, key_rows)
        softmax_f = jnp.exp(scores - log_total)
        prob_grad = jnp.einsum("the,she->hts", context_grad, value_rows, preferred_element_type=f32)
        score_grad = softmax_f * (
            prob_grad - jnp.sum(prob_grad * softmax_f, axis=-1, keepdims=True)
        )
        score_grad = score_grad.astype(jnp.bfloat16)
        query_grad = (
            jnp.einsum("hts,she->the", score_grad, key_rows, preferred_element_type=f32)
            * score_scale
        )
        key_grad = (
            jnp.einsum("hts,the->she", score_grad, queries, preferred_element_type=f32)
            * score_scale
        )
        value_grad = jnp.einsum(
            "hts,the->she", softmax_f.astype(jnp.bfloat16), context_grad, preferred_element_type=f32
        )
        query_grad, key_grad, value_grad = (
            grad.astype(jnp.bfloat16).reshape(row_count, local_width)
            for grad in (query_grad, key_grad, value_grad)
        )
        attn_sum = dp_share(
            *(
                jnp.einsum("td,tn->dn", normed, grad, preferred_element_type=f32)
                for grad in (query_grad, key_grad, value_grad)
            ),
            out_w_grad,
        )
        qv_bias_grad = jnp.stack(
            [jnp.sum(query_grad.astype(f32), axis=0), jnp.sum(value_grad.astype(f32), axis=0)]
        )
        qkv_grad = jnp.stack([query_grad, key_grad, value_grad])
        normed_grad = input_total(
            jnp.einsum("ctn,cdn->td", qkv_grad, w_rows[layer_idx], preferred_element_type=f32)
        )
        enter_grad, gain_attn, shift_attn = norm_back(
            entering, norm_gains[layer_idx, 0], norm_biases[layer_idx, 0], normed_grad
        )
        grad_rows = grad_rows + enter_grad
        small_parts.append(
            (
                jnp.stack([gain_attn, gain_mlp]),
                jnp.stack([shift_attn, shift_mlp]),
                jnp.stack([out_bias_grad, down_bias_grad]),
                qv_bias_grad,
                up_bias_grad,
            )
        )
        width = 3 * local_width
        hidden = w_up.shape[2]
        heavy = (
            attn_sum[:, :width].astype(f32).reshape(-1, 3, local_width),
            attn_sum[:, width:].astype(f32).T,
            mlp_sum[:, :hidden].astype(f32),
            mlp_sum[:, hidden:].astype(f32).T,
        )
        heavy_parts.append(heavy)
    small_parts = small_parts[::-1]
    heavy_parts = heavy_parts[::-1]
    gain_grads = jnp.stack([entry[0] for entry in small_parts])
    shift_grads = jnp.stack([entry[1] for entry in small_parts])
    bias_grads = jnp.stack([entry[2] for entry in small_parts])
    qv_grads = jnp.stack([entry[3] for entry in small_parts])
    up_bias_grads = jnp.stack([entry[4] for entry in small_parts])
    pieces = (gain_grads, shift_grads, bias_grads, qv_grads, up_bias_grads)
    flat = jnp.concatenate([piece.reshape(-1) for piece in pieces])
    unit = 16 * 1024
    flat = jnp.pad(flat, (0, -flat.size % unit)).astype(jnp.bfloat16).reshape(-1, 1024)
    flat = small_sum(flat, n_dp).reshape(-1)
    summed = []
    offset = 0
    for piece in pieces:
        summed.append(flat[offset : offset + piece.size].reshape(piece.shape))
        offset += piece.size
    gain_grads, shift_grads, bias_grads, qv_grads, up_bias_grads = summed
    qkv_all = jnp.stack([entry[0] for entry in heavy_parts])
    out_all = jnp.stack([entry[1] for entry in heavy_parts])
    up_all = jnp.stack([entry[2] for entry in heavy_parts])
    down_all = jnp.stack([entry[3] for entry in heavy_parts])
    return (
        block_rows,
        grad_rows,
        gain_grads,
        shift_grads,
        qkv_all,
        qv_grads,
        out_all,
        bias_grads,
        up_all,
        up_bias_grads,
        down_all,
    )


def solution(mesh):
    in_specs = (
        P("dp", None),
        P("dp", None),
        P("dp", None),
        P(),
        P(),
        P(None, None, None, "tensor"),
        P(None, None, "tensor"),
        P(None, "tensor", None),
        P(),
        P(None, None, "tensor"),
        P(None, "tensor"),
        P(None, "tensor", None),
    )
    out_specs = (
        P("dp", None),
        P("dp", None),
        P(),
        P(),
        P(None, "dp", None, "tensor"),
        P(None, None, "tensor"),
        P(None, "tensor", "dp"),
        P(),
        P(None, "dp", "tensor"),
        P(None, "tensor"),
        P(None, "tensor", "dp"),
    )
    return jax.shard_map(
        functools.partial(on_device, mesh.shape["dp"], mesh.shape["tensor"]), mesh=mesh, in_specs=in_specs, out_specs=out_specs, check_vma=False
    )
```

```python
import functools

import jax
import jax.numpy as jnp
from jax import lax
from jax.experimental import pallas as pl
from jax.experimental.pallas import tpu as pltpu
from jax.sharding import PartitionSpec as P


HEADS = 16
HEAD_DIM = 64


NORM_EPS = 1e-05


def layer_norm(residual, gain_vec, shift_vec):
    mean_row = jnp.mean(residual, axis=-1, keepdims=True)
    centered = residual - mean_row
    variance = jnp.mean(centered * centered, axis=-1, keepdims=True)
    return centered * lax.rsqrt(variance + NORM_EPS) * gain_vec + shift_vec


def gelu_tanh(pre_act):
    return (
        0.5
        * pre_act
        * (1.0 + jnp.tanh(0.7978845608028654 * (pre_act + 0.044715 * pre_act * pre_act * pre_act)))
    )


def norm_back(residual, gain_vec, shift_vec, grad_normed):
    result, pull_back = jax.vjp(layer_norm, residual, gain_vec, shift_vec)
    return pull_back(grad_normed)


def segment_mask(lengths, row_count):
    seq_ends = jnp.cumsum(lengths)
    position = jnp.arange(row_count, dtype=jnp.int32)
    segment = jnp.sum((position[:, None] >= seq_ends[None, :]).astype(jnp.int32), axis=1)
    same_seq = (segment[:, None] == segment[None, :]) & (position[None, :] <= position[:, None])
    row_gap = (position[:, None] - position[None, :]).astype(jnp.float32)
    live_rows = (position < seq_ends[-1]).astype(jnp.float32)
    return (same_seq, row_gap, live_rows)


MESH = pl.DeviceIdType.MESH
LAG = 3


def line_sum_kernel(n, p_ref, out_ref, rin, up, rx, up_send, in_recv, x_recv, out_send, out_recv):
    chunks = p_ref.shape[0]
    half = n // 2
    me = lax.axis_index("tensor")
    side = me // half
    step = 1 - 2 * side
    inward = me + step
    outward = me - step
    depth = side * (n - 1) + me * step

    barrier = pltpu.get_barrier_semaphore()
    pl.semaphore_signal(barrier, inc=1, device_id={"tensor": inward}, device_id_type=MESH)

    @pl.when(depth > 0)
    def _():
        pl.semaphore_signal(barrier, inc=1, device_id={"tensor": outward}, device_id_type=MESH)
        pl.semaphore_wait(barrier, 2)

    @pl.when(depth == 0)
    def _():
        pl.semaphore_wait(barrier, 1)

    def copy(source, target, send, recv, c, device):
        return pltpu.make_async_remote_copy(
            src_ref=source.at[c],
            dst_ref=target.at[c],
            send_sem=send.at[c],
            recv_sem=recv.at[c],
            device_id={"tensor": device},
            device_id_type=MESH,
        )

    def loop(body, start=0, stop=chunks):
        lax.fori_loop(start, stop, lambda c, carry: (body(c), carry)[1], 0)

    f32 = jnp.float32

    for role in range(half):
        depth_zero = role == 0
        middle = role == half - 1
        target, target_sem = (rx, x_recv) if middle else (rin, in_recv)
        source = p_ref if depth_zero else up

        def rise(c, depth_zero=depth_zero, source=source, target=target, target_sem=target_sem):
            if not depth_zero:
                copy(rin, rin, up_send, in_recv, c, outward).wait_recv()
                up[c] = (p_ref[c].astype(f32) + rin[c].astype(f32)).astype(up.dtype)
            copy(source, target, up_send, target_sem, c, inward).start()

        def fall(c, depth_zero=depth_zero, middle=middle, source=source):
            if middle:
                copy(rx, rx, up_send, x_recv, c, inward).wait_recv()
                out_ref[c] = (source[c].astype(f32) + rx[c].astype(f32)).astype(out_ref.dtype)
            else:
                copy(out_ref, out_ref, out_send, out_recv, c, inward).wait_recv()
            if not depth_zero:
                copy(out_ref, out_ref, out_send, out_recv, c, outward).start()

        def drain(c, depth_zero=depth_zero, source=source, target=target, target_sem=target_sem):
            copy(source, target, up_send, target_sem, c, inward).wait_send()
            if not depth_zero:
                copy(out_ref, out_ref, out_send, out_recv, c, outward).wait_send()

        @pl.when(depth == role)
        def _(middle=middle, rise=rise, fall=fall, drain=drain):
            if middle:
                loop(rise, 0, LAG)

                def both(c):
                    rise(c)
                    fall(c - LAG)

                loop(both, LAG, chunks)
                loop(fall, chunks - LAG, chunks)
            else:
                loop(rise)
                loop(fall)
            loop(drain)


def line_sum(partial, n, first_id=0):
    rows, width = partial.shape
    chunks = rows // 32
    shape = (chunks, rows // chunks, width)
    scratch = pltpu.VMEM(shape, partial.dtype)
    sems = pltpu.SemaphoreType.DMA((chunks,))
    out = pl.pallas_call(
        functools.partial(line_sum_kernel, n),
        out_shape=jax.ShapeDtypeStruct(shape, partial.dtype),
        in_specs=[pl.BlockSpec(memory_space=pltpu.VMEM)],
        out_specs=pl.BlockSpec(memory_space=pltpu.VMEM),
        scratch_shapes=[scratch, scratch, scratch, sems, sems, sems, sems, sems],
        compiler_params=pltpu.CompilerParams(
            collective_id=first_id, has_side_effects=True, vmem_limit_bytes=24 << 20
        ),
        cost_estimate=pl.CostEstimate(
            flops=rows * width * 60000, bytes_accessed=2 * rows * width * 2, transcendentals=0
        ),
        name="line_sum",
    )(partial.reshape(shape))
    return out.reshape(rows, width)


def small_sum_kernel(n, v_ref, out_ref, slots, send, recv):
    me = lax.axis_index("dp")
    barrier = pltpu.get_barrier_semaphore()
    for k in range(1, n):
        pl.semaphore_signal(
            barrier, inc=1, device_id={"dp": lax.rem(me + k, n)}, device_id_type=MESH
        )
    pl.semaphore_wait(barrier, n - 1)
    copies = []
    for k in range(1, n):
        copies.append(
            pltpu.make_async_remote_copy(
                src_ref=v_ref,
                dst_ref=slots.at[me],
                send_sem=send.at[k],
                recv_sem=recv.at[k],
                device_id={"dp": lax.rem(me + k, n)},
                device_id_type=MESH,
            )
        )
        copies[-1].start()
    slots[me] = v_ref[...]
    for k in range(1, n):
        pltpu.make_async_remote_copy(
            src_ref=v_ref,
            dst_ref=slots.at[lax.rem(me + n - k, n)],
            send_sem=send.at[k],
            recv_sem=recv.at[k],
            device_id={"dp": lax.rem(me + k, n)},
            device_id_type=MESH,
        ).wait_recv()
    total = slots[0].astype(jnp.float32)
    for k in range(1, n):
        total = total + slots[k].astype(jnp.float32)
    out_ref[...] = total
    for one in copies:
        one.wait_send()


def small_sum(values, n):
    return pl.pallas_call(
        functools.partial(small_sum_kernel, n),
        out_shape=jax.ShapeDtypeStruct(values.shape, jnp.float32),
        in_specs=[pl.BlockSpec(memory_space=pltpu.VMEM)],
        out_specs=pl.BlockSpec(memory_space=pltpu.VMEM),
        scratch_shapes=[
            pltpu.VMEM((n,) + values.shape, values.dtype),
            pltpu.SemaphoreType.DMA((n,)),
            pltpu.SemaphoreType.DMA((n,)),
        ],
        compiler_params=pltpu.CompilerParams(
            collective_id=1, has_side_effects=True, vmem_limit_bytes=8 << 20
        ),
        name="small_sum",
    )(values)


def weight_grads_kernel(spans, *refs):
    out_ref = refs[-1]
    for index, (start, width) in enumerate(spans):
        out_ref[:, start : start + width] = lax.dot_general(
            refs[2 * index][...],
            refs[2 * index + 1][...],
            (((0,), (0,)), ((), ())),
            preferred_element_type=jnp.float32,
        ).astype(out_ref.dtype)


def weight_grads(pairs):
    rows, height = pairs[0][0].shape
    block = min(256, height)
    spans, specs, operands, width = [], [], [], 0
    for left, right in pairs:
        spans.append((width, right.shape[1]))
        width += right.shape[1]
        specs.append(pl.BlockSpec((rows, block), lambda i: (0, i)))
        specs.append(pl.BlockSpec(right.shape, lambda i: (0, 0)))
        operands += [left, right]
    return pl.pallas_call(
        functools.partial(weight_grads_kernel, tuple(spans)),
        grid=(height // block,),
        out_shape=jax.ShapeDtypeStruct((height, width), jnp.bfloat16),
        in_specs=specs,
        out_specs=pl.BlockSpec((block, width), lambda i: (i, 0)),
        compiler_params=pltpu.CompilerParams(vmem_limit_bytes=24 << 20),
        cost_estimate=pl.CostEstimate(
            flops=2 * rows * height * width,
            bytes_accessed=2 * height * width + 8 * rows * height,
            transcendentals=0,
        ),
        name="weight_grads",
    )(*operands)


def on_device(
    n_dp,
    n_tensor,
    block_input,
    cotangent,
    seq_lengths,
    norm_gains,
    norm_biases,
    w_qkv,
    qv_bias,
    w_out,
    out_biases,
    w_up,
    up_bias,
    w_down,
):
    row_count = block_input.shape[0]
    my_rank = lax.axis_index("tensor")
    local_width = w_qkv.shape[3]
    heads_here = local_width // HEAD_DIM
    depth = w_qkv.shape[0]
    score_scale = HEAD_DIM ** (-0.5)
    f32 = jnp.float32
    same_seq, row_gap, live_rows = segment_mask(seq_lengths[0], row_count)
    head_index = my_rank * heads_here + jnp.arange(heads_here, dtype=jnp.int32) + 1
    slopes = jnp.exp2(-8.0 * head_index.astype(f32) / HEADS)

    def branch_total(partial_value):
        return line_sum(partial_value.astype(jnp.bfloat16), n_tensor).astype(jnp.float32)

    def input_total(partial_value):
        return line_sum(partial_value.astype(jnp.bfloat16), n_tensor).astype(jnp.float32)

    def dp_share(joined):
        return lax.psum_scatter(joined, "dp", scatter_dimension=0, tiled=True)

    def score_block(queries, key_rows):
        raw_scores = (
            jnp.einsum("the,she->hts", queries, key_rows, preferred_element_type=f32) * score_scale
        )
        raw_scores = raw_scores - slopes[:, None, None] * row_gap
        return jnp.where(same_seq, raw_scores, -1000000000.0)

    head_shape = (row_count, heads_here, HEAD_DIM)
    residual = block_input.astype(f32)
    stored = []
    for layer_idx in range(depth):
        entering = residual
        normed = layer_norm(residual, norm_gains[layer_idx, 0], norm_biases[layer_idx, 0]).astype(
            jnp.bfloat16
        )
        projected = jnp.einsum("td,dcn->tcn", normed, w_qkv[layer_idx], preferred_element_type=f32)
        queries = (projected[:, 0] + qv_bias[layer_idx, 0]).astype(jnp.bfloat16).reshape(head_shape)
        key_rows = projected[:, 1].astype(jnp.bfloat16).reshape(head_shape)
        value_rows = (
            (projected[:, 2] + qv_bias[layer_idx, 1]).astype(jnp.bfloat16).reshape(head_shape)
        )
        scores = score_block(queries, key_rows)
        row_max = jnp.max(scores, axis=-1, keepdims=True)
        log_total = row_max + jnp.log(jnp.sum(jnp.exp(scores - row_max), axis=-1, keepdims=True))
        softmax_p = jnp.exp(scores - log_total).astype(jnp.bfloat16)
        context = jnp.einsum("hts,she->the", softmax_p, value_rows, preferred_element_type=f32)
        context = context.astype(jnp.bfloat16).reshape(row_count, local_width)
        partial_value = jnp.dot(context, w_out[layer_idx], preferred_element_type=f32)
        residual = residual + branch_total(partial_value) + out_biases[layer_idx, 0]
        middle = residual
        normed_mlp = layer_norm(
            residual, norm_gains[layer_idx, 1], norm_biases[layer_idx, 1]
        ).astype(jnp.bfloat16)
        up_proj = (
            jnp.dot(normed_mlp, w_up[layer_idx], preferred_element_type=f32) + up_bias[layer_idx]
        )
        activated = gelu_tanh(up_proj).astype(jnp.bfloat16)
        partial_value = jnp.dot(activated, w_down[layer_idx], preferred_element_type=f32)
        if layer_idx == depth - 1:
            last_partial = partial_value.astype(jnp.bfloat16)
        else:
            residual = residual + branch_total(partial_value) + out_biases[layer_idx, 1]
        stored.append(
            (
                entering,
                normed,
                queries,
                key_rows,
                value_rows,
                log_total,
                context,
                middle,
                normed_mlp,
                up_proj,
                activated,
            )
        )
    grad_rows = cotangent.astype(f32) * live_rows[:, None]
    small_parts = []
    heavy_sums = []
    waiting = jnp.zeros((), jnp.bfloat16)
    for layer_idx in reversed(range(depth)):
        (
            entering,
            normed,
            queries,
            key_rows,
            value_rows,
            log_total,
            context,
            middle,
            normed_mlp,
            up_proj,
            activated,
        ) = stored[layer_idx]
        down_bias_grad = jnp.sum(grad_rows, axis=0)
        grad_low = grad_rows.astype(jnp.bfloat16)
        act_grad = jnp.einsum("td,fd->tf", grad_low, w_down[layer_idx], preferred_element_type=f32)
        up_grad = jax.vjp(gelu_tanh, up_proj)[1](act_grad)[0].astype(jnp.bfloat16)
        up_bias_grad = jnp.sum(up_grad.astype(f32), axis=0)
        joined = weight_grads(((normed_mlp, up_grad), (grad_low, activated)))
        partial_value = jnp.einsum(
            "tf,df->td", up_grad, w_up[layer_idx], preferred_element_type=f32
        ).astype(jnp.bfloat16)
        partial_value, joined, waiting = lax.optimization_barrier((partial_value, joined, waiting))
        if layer_idx < depth - 1:
            heavy_sums[-1] = waiting
        waiting = dp_share(joined)
        heavy_sums.append(waiting)
        if layer_idx == depth - 1:
            both = jnp.concatenate([partial_value, last_partial])
            both = line_sum(both, n_tensor, 2).astype(f32)
            normed_grad = both[:row_count]
            block_rows = residual + both[row_count:] + out_biases[layer_idx, 1]
            block_rows = block_rows.astype(jnp.bfloat16)
        else:
            normed_grad = input_total(partial_value)
        middle_grad, gain_mlp, shift_mlp = norm_back(
            middle, norm_gains[layer_idx, 1], norm_biases[layer_idx, 1], normed_grad
        )
        grad_rows = grad_rows + middle_grad
        out_bias_grad = jnp.sum(grad_rows, axis=0)
        grad_low = grad_rows.astype(jnp.bfloat16)
        context_grad = jnp.einsum(
            "td,nd->tn", grad_low, w_out[layer_idx], preferred_element_type=f32
        )
        context_grad = context_grad.astype(jnp.bfloat16).reshape(head_shape)
        scores = score_block(queries, key_rows)
        softmax_f = jnp.exp(scores - log_total)
        prob_grad = jnp.einsum("the,she->hts", context_grad, value_rows, preferred_element_type=f32)
        score_grad = softmax_f * (
            prob_grad - jnp.sum(prob_grad * softmax_f, axis=-1, keepdims=True)
        )
        score_grad = score_grad.astype(jnp.bfloat16)
        query_grad = (
            jnp.einsum("hts,she->the", score_grad, key_rows, preferred_element_type=f32)
            * score_scale
        )
        key_grad = (
            jnp.einsum("hts,the->she", score_grad, queries, preferred_element_type=f32)
            * score_scale
        )
        value_grad = jnp.einsum(
            "hts,the->she", softmax_f.astype(jnp.bfloat16), context_grad, preferred_element_type=f32
        )
        query_grad, key_grad, value_grad = (
            grad.astype(jnp.bfloat16).reshape(row_count, local_width)
            for grad in (query_grad, key_grad, value_grad)
        )
        joined = weight_grads(
            (
                (normed, query_grad),
                (normed, key_grad),
                (normed, value_grad),
                (grad_low, context),
            )
        )
        qv_bias_grad = jnp.stack(
            [jnp.sum(query_grad.astype(f32), axis=0), jnp.sum(value_grad.astype(f32), axis=0)]
        )
        qkv_grad = jnp.stack([query_grad, key_grad, value_grad], axis=1)
        partial_value = jnp.einsum(
            "tcn,dcn->td", qkv_grad, w_qkv[layer_idx], preferred_element_type=f32
        ).astype(jnp.bfloat16)
        partial_value, joined, waiting = lax.optimization_barrier((partial_value, joined, waiting))
        heavy_sums[-1] = waiting
        waiting = dp_share(joined)
        heavy_sums.append(waiting)
        normed_grad = input_total(partial_value)
        enter_grad, gain_attn, shift_attn = norm_back(
            entering, norm_gains[layer_idx, 0], norm_biases[layer_idx, 0], normed_grad
        )
        grad_rows = grad_rows + enter_grad
        small_parts.append(
            (
                jnp.stack([gain_attn, gain_mlp]),
                jnp.stack([shift_attn, shift_mlp]),
                jnp.stack([out_bias_grad, down_bias_grad]),
                qv_bias_grad,
                up_bias_grad,
            )
        )
    small_parts = small_parts[::-1]
    width = 3 * local_width
    hidden = w_up.shape[2]
    heavy_parts = []
    for mlp_sum, attn_sum in zip(heavy_sums[-2::-2], heavy_sums[-1::-2]):
        heavy_parts.append(
            (
                attn_sum[:, :width].astype(f32).reshape(-1, 3, local_width),
                attn_sum[:, width:].astype(f32).T,
                mlp_sum[:, :hidden].astype(f32),
                mlp_sum[:, hidden:].astype(f32).T,
            )
        )
    gain_grads = jnp.stack([entry[0] for entry in small_parts])
    shift_grads = jnp.stack([entry[1] for entry in small_parts])
    bias_grads = jnp.stack([entry[2] for entry in small_parts])
    qv_grads = jnp.stack([entry[3] for entry in small_parts])
    up_bias_grads = jnp.stack([entry[4] for entry in small_parts])
    pieces = (gain_grads, shift_grads, bias_grads, qv_grads, up_bias_grads)
    flat = jnp.concatenate([piece.reshape(-1) for piece in pieces])
    unit = 16 * 1024
    flat = jnp.pad(flat, (0, -flat.size % unit)).astype(jnp.bfloat16).reshape(-1, 1024)
    flat = small_sum(flat, n_dp).reshape(-1)
    summed = []
    offset = 0
    for piece in pieces:
        summed.append(flat[offset : offset + piece.size].reshape(piece.shape))
        offset += piece.size
    gain_grads, shift_grads, bias_grads, qv_grads, up_bias_grads = summed
    qkv_all = jnp.stack([entry[0] for entry in heavy_parts])
    out_all = jnp.stack([entry[1] for entry in heavy_parts])
    up_all = jnp.stack([entry[2] for entry in heavy_parts])
    down_all = jnp.stack([entry[3] for entry in heavy_parts])
    return (
        block_rows,
        grad_rows,
        gain_grads,
        shift_grads,
        qkv_all,
        qv_grads,
        out_all,
        bias_grads,
        up_all,
        up_bias_grads,
        down_all,
    )


def solution(mesh):
    in_specs = (
        P("dp", None),
        P("dp", None),
        P("dp", None),
        P(),
        P(),
        P(None, None, None, "tensor"),
        P(None, None, "tensor"),
        P(None, "tensor", None),
        P(),
        P(None, None, "tensor"),
        P(None, "tensor"),
        P(None, "tensor", None),
    )
    out_specs = (
        P("dp", None),
        P("dp", None),
        P(),
        P(),
        P(None, "dp", None, "tensor"),
        P(None, None, "tensor"),
        P(None, "tensor", "dp"),
        P(),
        P(None, "dp", "tensor"),
        P(None, "tensor"),
        P(None, "tensor", "dp"),
    )
    return jax.shard_map(
        functools.partial(on_device, mesh.shape["dp"], mesh.shape["tensor"]), mesh=mesh, in_specs=in_specs, out_specs=out_specs, check_vma=False
    )
```
